256 devices in a mesh: wide: 32 (over x, y, core), narrow: 8 (over z).
Axes of the slice: x: 4, y: 4, z: 8, core: 2. Of those that a mesh axis runs over, the one named last changes fastest.
Arguments:
- momentum: float32 [9216, 9216], P('wide', 'narrow'), may hold values from -3 to 3
- gradient: bfloat16 [9216, 9216], P('wide', 'narrow'), may hold values from -48 to 48
- right_factor: float32 [512, 9216], P('wide', 'narrow'), may hold values from -6 to 6
Outputs:
- new_momentum: float32 [9216, 9216], P('wide', 'narrow')
- new_right: float32 [512, 9216], P('wide', 'narrow')
- update: bfloat16 [9216, 9216], P('wide', 'narrow')
The draws below stay inside these ranges and needn't reach their ends.
All inputs are finite; a program needn't handle non-finite values.
Results may differ from the reference program's by a relative error of at most 0.001.
Values sent between devices are 32-bit elements; how exact they have to be, the bound alone decides.
A program may use at most 64 MiB of HBM per device.

```python
import math
import jax
import jax.numpy as jnp
from jax import lax

M_ROWS = 9216
N_COLS = 9216
RANK = 512


def draw_gradient(key, part):
    keys = jax.random.split(jax.random.fold_in(key, 17), 3)
    row_place = jnp.arange(M_ROWS, dtype=jnp.float32) / M_ROWS
    col_place = jnp.arange(N_COLS, dtype=jnp.float32) / N_COLS
    row_rough = jnp.exp(jax.random.uniform(keys[0], (M_ROWS,), jnp.float32, math.log(0.4), math.log(2.5)))
    col_rough = jnp.exp(jax.random.uniform(keys[1], (N_COLS,), jnp.float32, math.log(0.4), math.log(2.5)))
    noise = jnp.clip(jax.random.normal(keys[2], (M_ROWS, N_COLS), jnp.float32), -4.0, 4.0)
    row_trend = 3.0 ** (row_place - 0.5)
    col_trend = 3.0 ** (col_place - 0.5)
    values = noise * (row_trend * row_rough)[:, None] * (col_trend * col_rough)[None, :]
    return jnp.clip(values, -48.0, 48.0).astype(jnp.bfloat16)


def steps_of(stream_key, shape, cuts, smallest, high):
    loudness, own = 1.0, jax.random.fold_in(stream_key, 6)
    for dim, parts in cuts:
        steps = jnp.exp(jax.random.uniform(jax.random.fold_in(own, dim), (parts,), jnp.float32, smallest / len(cuts), high / len(cuts)))
        loudness = loudness * jnp.repeat(steps, shape[dim] // parts).reshape([-1 if axis == dim else 1 for axis in range(len(shape))])
    return loudness


def normal_values(key, extent, spread, reach, cuts=(), kind=jnp.bfloat16):
    gain = steps_of(key, extent, cuts, -0.22, 0.18) if cuts else 1.0
    result = jax.random.normal(key, extent, jnp.float32) * spread * gain
    return jnp.minimum(jnp.maximum(result, -reach), reach).astype(kind)


def setup_inputs(seed: int = 0) -> dict:
    key_of = jax.random.split(jax.random.key(seed), 4)
    momentum = normal_values(key_of[0], (M_ROWS, N_COLS), 0.5, 3.0, ((0, 32), (1, 8)), jnp.float32)
    gradient = draw_gradient(jax.random.fold_in(key_of[3], 71), 0)
    right_factor = normal_values(key_of[2], (RANK, N_COLS), 1.0, 6.0, ((0, 32), (1, 8)), jnp.float32)
    return {"momentum": momentum, "gradient": gradient, "right_factor": right_factor}


EPS = 1e-06
MU = 0.95

def orthonormal(projected, gram_matrix):
    factor_lower = jnp.linalg.cholesky(gram_matrix)
    return jax.scipy.linalg.solve_triangular(factor_lower, projected.T, lower=True).T

def reference(momentum, gradient, right_factor):
    precise = lax.Precision.HIGHEST
    blended = momentum + gradient.astype(jnp.float32)
    projected = jnp.dot(blended.astype(jnp.float32), right_factor.T.astype(jnp.float32), preferred_element_type=jnp.float32, precision=precise)
    gram_matrix = jnp.dot(projected.T.astype(jnp.float32), projected.astype(jnp.float32), preferred_element_type=jnp.float32, precision=precise)
    left_basis = orthonormal(projected, gram_matrix)
    right_sums = jnp.dot(left_basis.T.astype(jnp.float32), blended.astype(jnp.float32), preferred_element_type=jnp.float32, precision=precise)
    root_mean = jnp.sqrt(lax.optimization_barrier(jnp.sum(right_sums * right_sums, axis=1)) / N_COLS + EPS)
    new_right = right_sums / root_mean[:, None]
    feedback = jnp.dot(left_basis.astype(jnp.float32), right_sums.astype(jnp.float32), preferred_element_type=jnp.float32, precision=precise)
    new_momentum = blended - (1.0 - MU) * feedback
    direction = jnp.dot(left_basis.astype(jnp.float32), new_right.astype(jnp.float32), preferred_element_type=jnp.float32, precision=precise)
    return (new_momentum, new_right, direction.astype(jnp.bfloat16))
```

```python
import jax
import jax.numpy as jnp
from jax import lax
from jax.experimental import pallas as pl
from jax.experimental.pallas import tpu as pltpu
from jax.sharding import Mesh
from jax.sharding import PartitionSpec as P

N_COLS = 9216
WIDE = ("wide_0", "wide_1", "wide_2")


EPS = 1e-06
MU = 0.95


def sent_to_all(value, axis):
    copies = jnp.broadcast_to(value, (lax.axis_size(axis), *value.shape))
    return lax.all_to_all(copies, axis, split_axis=0, concat_axis=0, tiled=True)


def in_order(parts, dim):
    parts = jnp.moveaxis(parts, 0, dim)
    dims = parts.shape
    return parts.reshape(*dims[:dim], dims[dim] * dims[dim + 1], *dims[dim + 2 :])


def whole_of(value, axes, dim):
    far, near = axes
    parts = sent_to_all(sent_to_all(value, far), near)
    return in_order(parts.swapaxes(0, 1).reshape(-1, *value.shape), dim)


def filled_up(lines, count):
    spare = -len(lines) % count
    return jnp.pad(lines, [(0, spare)] + [(0, 0)] * (lines.ndim - 1))


def sum_by_parts(value, axis):
    lines = value.reshape(-1, *value.shape[1:][-1:])
    padded = filled_up(lines, lax.axis_size(axis))
    own = lax.psum_scatter(padded, axis, scatter_dimension=0, tiled=True)
    whole = lax.all_gather(own, axis, axis=0, tiled=True)
    return whole[: len(lines)].reshape(value.shape)


def cut_along(value, dim, count):
    dims = value.shape
    parts = value.reshape(*dims[:dim], count, dims[dim] // count, *dims[dim + 1 :])
    return jnp.moveaxis(parts, dim, 0)


def summed_on_arrival(value, axis, dim):
    count = lax.axis_size(axis)
    parts = lax.all_to_all(cut_along(value, dim, count), axis, 0, 0, tiled=True)
    return jnp.sum(parts, axis=0)


def summed_rows(value, axes, dim):
    far, near = axes
    parts = cut_along(value, dim, lax.axis_size(far))
    nearer = summed_on_arrival(parts, near, dim + 1)
    arrived = lax.all_to_all(nearer, far, split_axis=0, concat_axis=0, tiled=True)
    return arrived.sum(axis=0)


def nested_sum(value, axes):
    lines = value.reshape(-1, value.shape[-1])
    own = summed_rows(filled_up(lines, lax.axis_size(axes[0]) * lax.axis_size(axes[1])), axes, 0)
    whole = whole_of(own, axes, 0)
    return whole[: len(lines)].reshape(value.shape)


def taken_together(value, axis):
    return sent_to_all(value, axis).sum(axis=0)


def sent_together(arrays, axis, dim, along):
    columns = [a.reshape(*a.shape[:along], -1) for a in arrays]
    both = jnp.concatenate(columns, axis=along)
    filled, at, finished = (lax.all_gather(both, axis, axis=dim, tiled=True), 0, [])
    for a, column in zip(arrays, columns):
        slab = filled[..., at : at + column.shape[along]]
        finished.append(slab.reshape(*slab.shape[:along], *a.shape[along:]))
        at += column.shape[along]
    return tuple(finished)


HI = lax.Precision.HIGHEST

def lane_of(tile, lane):
    return jnp.broadcast_to(tile[:, lane:lane + 1], tile.shape)

def row_of(tile, row):
    return jnp.broadcast_to(tile[row:row + 1, :], tile.shape)

def inv_chol_block(d):
    n = 128
    tiles = [d[8 * i:8 * i + 8, :] for i in range(n // 8)]
    lanes = lax.broadcasted_iota(jnp.int32, (8, n), 1)
    subs = lax.broadcasted_iota(jnp.int32, (8, n), 0)
    for j in range(n // 8):
        t = tiles[j]
        inside = (lanes >= 8 * j) & (lanes < 8 * j + 8)
        cols = [lane_of(t, 8 * j + k) for k in range(8)]
        e = {(i, k): row_of(cols[k], i) for k in range(8) for i in range(k, 8)}
        raw = {i: [lane_of(tiles[i], 8 * j + k) for k in range(8)] for i in range(j + 1, n // 8)}
        own = jnp.where(inside, jnp.where(lanes - 8 * j == subs, 1.0, 0.0), t)
        rows = [row_of(own, k) for k in range(8)]
        scale, low = [], {}
        for k in range(8):
            scale.append(lax.rsqrt(e[k, k]))
            for i in range(k + 1, 8):
                low[i, k] = e[i, k] * scale[k]
            for i in range(k + 1, 8):
                for m in range(k + 1, i + 1):
                    e[i, m] = e[i, m] - low[i, k] * low[m, k]
        def forward(values):
            out = []
            for k in range(8):
                v = values[k]
                for m in range(k):
                    v = v - low[k, m] * out[m]
                out.append(v * scale[k])
            return out
        up = forward(rows)
        new = up[0]
        for k in range(1, 8):
            new = jnp.where(subs == k, up[k], new)
        tiles[j] = new
        for i in range(j + 1, n // 8):
            c = forward(raw[i])
            v = jnp.where(inside, 0.0, tiles[i])
            for k in range(8):
                v = v - c[k] * up[k]
            tiles[i] = v
    x = jnp.concatenate(tiles, axis=0)
    r = lax.broadcasted_iota(jnp.int32, (n, n), 0)
    c = lax.broadcasted_iota(jnp.int32, (n, n), 1)
    return jnp.where(c <= r, x, 0.0)

def dot_nt(a, b):
    return lax.dot_general(a, b, (((1,), (1,)), ((), ())), precision=HI, preferred_element_type=jnp.float32)

def dot_nn(a, b):
    return lax.dot_general(a, b, (((1,), (0,)), ((), ())), precision=HI, preferred_element_type=jnp.float32)

def inv_chol(m_ref, nb=4):
    b = 128
    for k in range(nb):
        s = slice(b * k, b * k + b)
        x = inv_chol_block(m_ref[s, s])
        if k:
            left = m_ref[s, :b * k]
            left = dot_nn(x, left)
            m_ref[s, :b * k] = left
        m_ref[s, s] = x
        for i in range(k + 1, nb):
            t = slice(b * i, b * i + b)
            c = dot_nt(m_ref[t, s], x)
            m_ref[t, s] = c
        for i in range(k + 1, nb):
            t = slice(b * i, b * i + b)
            c = m_ref[t, s]
            for q in range(k + 1, i + 1):
                u = slice(b * q, b * q + b)
                m_ref[t, u] = m_ref[t, u] - dot_nt(c, m_ref[u, s])
        for i in range(nb - 1, k, -1):
            t = slice(b * i, b * i + b)
            c = m_ref[t, s]
            if k:
                m_ref[t, :b * k] = m_ref[t, :b * k] - dot_nn(c, m_ref[s, :b * k])
            m_ref[t, s] = -dot_nn(c, x)
        if k:
            pass
    for k in range(nb):
        for q in range(k + 1, nb):
            m_ref[b * k:b * k + b, b * q:b * q + b] = jnp.zeros((b, b), jnp.float32)

def kernel(g_ref, x_ref):
    x_ref[...] = g_ref[...]
    inv_chol(x_ref)

def inverse_factor(g):
    return pl.pallas_call(
        kernel,
        out_shape=jax.ShapeDtypeStruct((512, 512), jnp.float32),
        in_specs=[pl.BlockSpec(memory_space=pltpu.VMEM)],
        out_specs=pl.BlockSpec(memory_space=pltpu.VMEM),
        compiler_params=pltpu.CompilerParams(vmem_limit_bytes=32 << 20),
    )(g)


def orthonormal(projected, gram_matrix):
    return dot_nt(projected, inverse_factor(gram_matrix))


def matmul(left, right):
    return jnp.dot(left, right, preferred_element_type=jnp.float32, precision=lax.Precision.HIGHEST)


def per_device(momentum, gradient, right_factor):
    blended = momentum + gradient.astype(jnp.float32)
    partial_left = matmul(blended, whole_of(right_factor, (("wide_0", "wide_1"), "wide_2"), 0).T)
    projected = sum_by_parts(partial_left, "narrow")
    gram_matrix = nested_sum(matmul(projected.T, projected), (("wide_0", "wide_1"), "wide_2"))
    left_basis = orthonormal(projected, gram_matrix)
    columns = left_basis
    right_block = summed_on_arrival(matmul(columns.T, blended), WIDE, 0)
    squares = taken_together(jnp.sum(right_block * right_block, axis=1), "narrow")
    root_mean = jnp.sqrt(squares / N_COLS + EPS)
    new_right = right_block / root_mean[:, None]
    pieces = sent_together((right_block, root_mean), WIDE, 0, 1)
    columns = left_basis
    normed = pieces[0] / pieces[1][:, None]
    feedback = matmul(columns, pieces[0])
    direction = matmul(columns, normed)
    new_momentum = blended - (1.0 - MU) * feedback
    return (new_momentum, new_right, direction.astype(jnp.bfloat16))


def solution(mesh):
    finer = Mesh(
        mesh.devices.reshape(4, 4, 2, mesh.shape["narrow"]),
        ("wide_0", "wide_1", "wide_2", "narrow"),
    )
    return jax.shard_map(
        per_device,
        mesh=finer,
        in_specs=(P(WIDE, "narrow"), P(WIDE, "narrow"), P(WIDE, "narrow")),
        out_specs=(P(WIDE, "narrow"), P(WIDE, "narrow"), P(WIDE, "narrow")),
        check_vma=False,
    )
```

```python
import functools
import jax
import jax.numpy as jnp
from jax import lax
from jax.experimental import pallas as pl
from jax.experimental.pallas import tpu as pltpu
from jax.sharding import Mesh
from jax.sharding import PartitionSpec as P

N_COLS = 9216
WIDE = ("wide_0", "wide_1", "wide_2")
EPS = 1e-06
MU = 0.95
HI = lax.Precision.HIGHEST
MESH = pl.DeviceIdType.MESH
ROWS, COLS, RANK, STRIP, BLOCK = 288, 1152, 512, 40, 128
PAIRS = [(i, j) for i in range(4) for j in range(i + 1)]


def dot(a, b, ca, cb):
    return lax.dot_general(a, b, (((ca,), (cb,)), ((), ())), precision=HI, preferred_element_type=jnp.float32)


def dot_nt(a, b):
    return dot(a, b, 1, 1)


def dot_nn(a, b):
    return dot(a, b, 1, 0)


def lane_of(tile, lane):
    return jnp.broadcast_to(tile[:, lane:lane + 1], tile.shape)

def row_of(tile, row):
    return jnp.broadcast_to(tile[row:row + 1, :], tile.shape)

def inv_chol_block(d):
    n = 128
    tiles = [d[8 * i:8 * i + 8, :] for i in range(n // 8)]
    lanes = lax.broadcasted_iota(jnp.int32, (8, n), 1)
    subs = lax.broadcasted_iota(jnp.int32, (8, n), 0)
    for j in range(n // 8):
        t = tiles[j]
        inside = (lanes >= 8 * j) & (lanes < 8 * j + 8)
        cols = [lane_of(t, 8 * j + k) for k in range(8)]
        e = {(i, k): row_of(cols[k], i) for k in range(8) for i in range(k, 8)}
        raw = {i: [lane_of(tiles[i], 8 * j + k) for k in range(8)] for i in range(j + 1, n // 8)}
        own = jnp.where(inside, jnp.where(lanes - 8 * j == subs, 1.0, 0.0), t)
        rows = [row_of(own, k) for k in range(8)]
        scale, low = [], {}
        for k in range(8):
            scale.append(lax.rsqrt(e[k, k]))
            for i in range(k + 1, 8):
                low[i, k] = e[i, k] * scale[k]
            for i in range(k + 1, 8):
                for m in range(k + 1, i + 1):
                    e[i, m] = e[i, m] - low[i, k] * low[m, k]
        def forward(values):
            out = []
            for k in range(8):
                v = values[k]
                for m in range(k):
                    v = v - low[k, m] * out[m]
                out.append(v * scale[k])
            return out
        up = forward(rows)
        new = up[0]
        for k in range(1, 8):
            new = jnp.where(subs == k, up[k], new)
        tiles[j] = new
        for i in range(j + 1, n // 8):
            c = forward(raw[i])
            v = jnp.where(inside, 0.0, tiles[i])
            for k in range(8):
                v = v - c[k] * up[k]
            tiles[i] = v
    x = jnp.concatenate(tiles, axis=0)
    r = lax.broadcasted_iota(jnp.int32, (n, n), 0)
    c = lax.broadcasted_iota(jnp.int32, (n, n), 1)
    return jnp.where(c <= r, x, 0.0)

def inv_chol(m_ref, hooks, nb=4):
    b = 128
    for k in range(nb):
        s = slice(b * k, b * k + b)
        x = inv_chol_block(m_ref[s, s])
        if k:
            left = m_ref[s, :b * k]
            left = dot_nn(x, left)
            m_ref[s, :b * k] = left
        m_ref[s, s] = x
        for i in range(k + 1, nb):
            t = slice(b * i, b * i + b)
            c = dot_nt(m_ref[t, s], x)
            m_ref[t, s] = c
        for i in range(k + 1, nb):
            t = slice(b * i, b * i + b)
            c = m_ref[t, s]
            for q in range(k + 1, i + 1):
                u = slice(b * q, b * q + b)
                m_ref[t, u] = m_ref[t, u] - dot_nt(c, m_ref[u, s])
        for i in range(nb - 1, k, -1):
            t = slice(b * i, b * i + b)
            c = m_ref[t, s]
            if k:
                m_ref[t, :b * k] = m_ref[t, :b * k] - dot_nn(c, m_ref[s, :b * k])
            m_ref[t, s] = -dot_nn(c, x)
        if k in hooks:
            hooks[k]()
    for k in range(nb):
        for q in range(k + 1, nb):
            m_ref[b * k:b * k + b, b * q:b * q + b] = jnp.zeros((b, b), jnp.float32)


def step_kernel(
    momentum, gradient, right, new_momentum, new_right, update,
    mom, grad, a, r_all, part, z_got, p_all, g_part, g_comb, g_half, g_got, g_z, g_all, m,
    w_part, w_comb, w_half, w_got, w_all, s, p, q, n_z, roots,
    local, r_s, r_r, rf_s, rf_r, z_s, z_r, p_s, p_r, gc_s, gc_r, gr_s, gr_r, gz_s, gz_r, ga_s, ga_r, gf_s, gf_r,
    wc_s, wc_r, wr_s, wr_r, wa_s, wa_r, wf_s, wf_r, nz_s, nz_r,
):
    x, y, c, z = (lax.axis_index(n) for n in (*WIDE, "narrow"))
    xy = x * 4 + y
    sibling = (x, y, 1 - c, z)

    def plane(t):
        return (lax.rem(x + t // 4, 4), lax.rem(y + lax.rem(t, 4), 4), c, z)

    def plane_from(t):
        return lax.rem(x + 4 - t // 4, 4) * 4 + lax.rem(y + 4 - lax.rem(t, 4), 4)

    def column(t):
        return (x, y, c, lax.rem(z + t, 8))

    def column_from(t):
        return lax.rem(z + 8 - t, 8)

    def remote(src, dst, send, recv, to):
        return pltpu.make_async_remote_copy(
            src_ref=src, dst_ref=dst, send_sem=send, recv_sem=recv, device_id=to, device_id_type=MESH
        )

    def loop(low, high, body):
        def run(i, carry):
            body(i)
            return carry

        lax.fori_loop(low, high, run, 0)

    loads = [
        pltpu.make_async_copy(right, r_all.at[x, y, c], local.at[0]),
        pltpu.make_async_copy(momentum, mom, local.at[1]),
        pltpu.make_async_copy(gradient, grad, local.at[2]),
    ]
    for load in loads:
        load.start()

    barrier = pltpu.get_barrier_semaphore()

    def hello(to):
        pl.semaphore_signal(barrier, inc=1, device_id=to, device_id_type=MESH)

    hello(sibling)
    loop(1, 16, lambda t: hello(plane(t)))
    loop(1, 8, lambda t: hello(column(t)))
    pl.semaphore_wait(barrier, 23)

    def r_send(t):
        return remote(r_all.at[x, y, c], r_all.at[x, y, c], r_s.at[t], r_r.at[t], plane(t))

    def r_wait(t):
        f = plane_from(t)
        block = r_all.at[f // 4, lax.rem(f, 4), c]
        remote(block, block, r_s.at[t], r_r.at[t], plane(t)).wait_recv()

    def r_forward(g):
        xg = lax.rem(x + 4 - g, 4)
        return remote(r_all.at[xg, :, c], r_all.at[xg, :, c], rf_s.at[g], rf_r.at[g], sibling)

    def r_forward_wait(g):
        xg = lax.rem(x + 4 - g, 4)
        remote(r_all.at[xg, :, 1 - c], r_all.at[xg, :, 1 - c], rf_s.at[g], rf_r.at[g], sibling).wait_recv()

    loads[0].wait()
    order = (0, 1, 3, 2)
    for g in order:
        loop(4 * g + (g == 0), 4 * g + 4, lambda t: r_send(t).start())
    loads[1].wait()
    loads[2].wait()
    a[...] = mom[...] + grad[...].astype(jnp.float32)

    def z_rows(t):
        return pl.ds(pl.multiple_of(8 * ((9 * t) // 2), 8), STRIP)

    def z_send(g, t):
        to = lax.rem(z + t, 8)
        xg = lax.rem(x + 4 - g, 4)
        return remote(part.at[xg, z_rows(to)], z_got.at[z, xg], z_s.at[g, t], z_r.at[g, t], column(t))

    def z_wait(g, t):
        f = column_from(t)
        xg = lax.rem(x + 4 - g, 4)
        remote(z_got.at[f, xg], z_got.at[f, xg], z_s.at[g, t], z_r.at[g, t], column(t)).wait_recv()

    def r_arrive(g):
        loop(4 * g + (g == 0), 4 * g + 4, r_wait)
        r_forward(g).start()

    r_arrive(order[0])
    for o in range(4):
        g = order[o]
        if o < 3:
            r_arrive(order[o + 1])
        r_forward_wait(g)
        xg = lax.rem(x + 4 - g, 4)
        ranks = r_all[pl.ds(xg, 1)].reshape(BLOCK, COLS)
        part[pl.ds(xg, 1)] = dot(a[...], ranks, 1, 1).reshape(1, ROWS, BLOCK)
        loop(1, 8, lambda t: z_send(g, t).start())
    for g in range(4):
        z_got[pl.ds(z, 1), pl.ds(g, 1)] = part[pl.ds(g, 1), z_rows(z)].reshape(1, 1, STRIP, BLOCK)
    for g in order:
        loop(1, 8, lambda t: z_wait(g, t))

    total = z_got[0]
    for t in range(1, 8):
        total = total + z_got[t]
    p_all[pl.ds(z, 1)] = total.reshape(1, 4, STRIP, BLOCK)

    def p_send(t):
        return remote(p_all.at[z], p_all.at[z], p_s.at[t], p_r.at[t], column(t))

    def p_wait(t):
        f = column_from(t)
        remote(p_all.at[f], p_all.at[f], p_s.at[t], p_r.at[t], column(t)).wait_recv()

    loop(1, 8, lambda t: p_send(t).start())

    tile_rows = lax.broadcasted_iota(jnp.int32, (STRIP, BLOCK), 0)
    fresh = (tile_rows >= 8) | (lax.rem(z, 2) == 0)
    own = [jnp.where(fresh, total[i], 0.0) for i in range(4)]
    pieces = []
    for i in range(4):
        wide = jnp.concatenate(own[: i + 1], axis=1)
        strip = dot(own[i], wide, 0, 0)
        pieces += [strip[:, BLOCK * j : BLOCK * j + BLOCK] for j in range(i + 1)]
    g_part[...] = jnp.concatenate(pieces, axis=0).reshape(16, 2, STRIP, BLOCK)

    g_swap = remote(g_part.at[:, 1 - c], g_comb, gc_s.at[0], gc_r.at[0], sibling)
    g_swap.start()
    g_swap.wait_recv()
    g_half[...] = g_part[:, pl.ds(c, 1)].reshape(16, STRIP, BLOCK) + g_comb[...]

    def g_send(t):
        tx, ty, _, _ = plane(t)
        return remote(g_half.at[tx * 4 + ty], g_got.at[t], gr_s.at[t], gr_r.at[t], plane(t))

    def g_wait(t):
        remote(g_got.at[t], g_got.at[t], gr_s.at[t], gr_r.at[t], plane(t)).wait_recv()

    loop(1, 16, lambda t: g_send(t).start())
    loop(1, 16, g_wait)
    strip = g_half[pl.ds(xy, 1)].reshape(STRIP, BLOCK)
    for t in range(1, 16):
        strip = strip + g_got[t]
    g_z[pl.ds(z, 1)] = strip.reshape(1, STRIP, BLOCK)

    def gz_send(t):
        return remote(g_z.at[z], g_z.at[z], gz_s.at[t], gz_r.at[t], column(t))

    def gz_wait(t):
        f = column_from(t)
        remote(g_z.at[f], g_z.at[f], gz_s.at[t], gz_r.at[t], column(t)).wait_recv()

    loop(1, 8, lambda t: gz_send(t).start())
    loop(1, 8, gz_wait)
    strip = g_z[0]
    for t in range(1, 8):
        strip = strip + g_z[t]
    g_all[pl.ds(xy, 1), pl.ds(c, 1)] = strip.reshape(1, 1, STRIP, BLOCK)

    def ga_send(t):
        return remote(g_all.at[xy, c], g_all.at[xy, c], ga_s.at[t], ga_r.at[t], plane(t))

    def ga_wait(t):
        f = plane_from(t)
        remote(g_all.at[f, c], g_all.at[f, c], ga_s.at[t], ga_r.at[t], plane(t)).wait_recv()

    loop(1, 16, lambda t: ga_send(t).start())

    loop(1, 8, p_wait)
    for t in range(8):
        first = (9 * t) // 2
        skip = t % 2
        for i in range(4):
            p[8 * (first + skip) : 8 * (first + 5), BLOCK * i : BLOCK * i + BLOCK] = p_all[t, i, 8 * skip :]
    for i in range(4):
        lanes = slice(BLOCK * i, BLOCK * i + BLOCK)
        w_part[4 * i : 4 * i + 4] = dot(p[:, lanes], a[...], 0, 0).reshape(4, 2, 16, COLS)
    w_swap = remote(w_part.at[:, 1 - c], w_comb, wc_s.at[0], wc_r.at[0], sibling)
    w_swap.start()

    loop(1, 16, ga_wait)
    g_forward = remote(g_all.at[:, c], g_all.at[:, c], gf_s.at[0], gf_r.at[0], sibling)
    g_forward.start()

    def w_send(t):
        tx, ty, _, _ = plane(t)
        return remote(w_half.at[tx * 4 + ty], w_got.at[t], wr_s.at[t], wr_r.at[t], plane(t))

    def w_wait(t):
        remote(w_got.at[t], w_got.at[t], wr_s.at[t], wr_r.at[t], plane(t)).wait_recv()

    def wa_send(t):
        return remote(w_all.at[xy, c], w_all.at[xy, c], wa_s.at[t], wa_r.at[t], plane(t))

    def wa_wait(t):
        f = plane_from(t)
        block = w_all.at[f // 4 * 4 + lax.rem(f, 4), c]
        remote(block, block, wa_s.at[t], wa_r.at[t], plane(t)).wait_recv()

    w_swap.wait_recv()
    w_half[...] = w_part[:, pl.ds(c, 1)].reshape(16, 16, COLS) + w_comb[...]
    loop(1, 16, lambda t: w_send(t).start())

    remote(g_all.at[:, 1 - c], g_all.at[:, 1 - c], gf_s.at[0], gf_r.at[0], sibling).wait_recv()
    for n, (i, j) in enumerate(PAIRS):
        for k in range(16):
            t = 16 * n + k
            o, e = divmod(t, 5)
            m[BLOCK * i + 8 * k : BLOCK * i + 8 * k + 8, BLOCK * j : BLOCK * j + BLOCK] = g_all[
                o // 2, o % 2, 8 * e : 8 * e + 8
            ]

    def w_sum():
        loop(1, 16, w_wait)
        got = w_half[pl.ds(xy, 1)].reshape(16, COLS)
        for t in range(1, 16):
            got = got + w_got[t]
        w_all[pl.ds(xy, 1), pl.ds(c, 1)] = got.reshape(1, 1, 16, COLS)
        loop(1, 16, lambda t: wa_send(t).start())

    def wf(v, g):
        rows = pl.ds(4 * g, 4)
        return remote(w_all.at[rows, v], w_all.at[rows, v], wf_s.at[g], wf_r.at[g], sibling)

    def w_forward():
        loop(1, 16, wa_wait)
        loop(0, 4, lambda g: wf(c, g).start())

    inv_chol(m, {W_SUM_AT: w_sum, W_FORWARD_AT: w_forward})

    for i in range(4):
        lanes = slice(BLOCK * i, BLOCK * i + BLOCK)
        q[:, lanes] = dot(p[:, : BLOCK * i + BLOCK], m[lanes, : BLOCK * i + BLOCK], 1, 1)
    loop(0, 4, lambda g: wf(1 - c, g).wait_recv())
    squares = jnp.zeros((8, RANK), jnp.float32)
    ones = jnp.ones((8, COLS), jnp.float32)
    for i in range(4):
        rows = slice(BLOCK * i, BLOCK * i + BLOCK)
        known = w_all[: 4 * i + 4].reshape(BLOCK * i + BLOCK, COLS)
        block = dot(m[rows, : BLOCK * i + BLOCK], known, 1, 0)
        s[8 * i : 8 * i + 8] = block.reshape(8, 16, COLS)
        n_z[pl.ds(z, 1), :, rows] = dot(ones, block * block, 1, 1).reshape(1, 8, BLOCK)

    def nz_send(t):
        return remote(n_z.at[z], n_z.at[z], nz_s.at[t], nz_r.at[t], column(t))

    def nz_wait(t):
        f = column_from(t)
        remote(n_z.at[f], n_z.at[f], nz_s.at[t], nz_r.at[t], column(t)).wait_recv()

    loop(1, 8, lambda t: nz_send(t).start())
    sums = s[...].reshape(RANK, COLS)
    new_momentum[...] = a[...] - (1.0 - MU) * dot(q[...], sums, 1, 0)
    loop(1, 8, nz_wait)
    squares = n_z[0]
    for t in range(1, 8):
        squares = squares + n_z[t]
    root = jnp.sqrt(squares / N_COLS + EPS)
    update[...] = dot(q[...] * (1.0 / root[:1]), sums, 1, 0).astype(jnp.bfloat16)
    for i in range(4):
        turned = jnp.broadcast_to(root[:1, BLOCK * i : BLOCK * i + BLOCK], (BLOCK, BLOCK)).T
        roots[8 * i : 8 * i + 8] = turned.reshape(8, 16, BLOCK)
    mine = xy * 2 + c
    scale = roots[pl.ds(mine, 1)].reshape(16, BLOCK)
    strip = s[pl.ds(mine, 1)].reshape(16, COLS)
    for k in range(9):
        new_right[:, BLOCK * k : BLOCK * k + BLOCK] = strip[:, BLOCK * k : BLOCK * k + BLOCK] / scale

    def sent(copy):
        copy.wait_send()

    loop(1, 16, lambda t: sent(r_send(t)))
    loop(0, 4, lambda g: sent(r_forward(g)))
    for g in range(4):
        loop(1, 8, lambda t: sent(z_send(g, t)))
    loop(1, 8, lambda t: sent(p_send(t)))
    sent(g_swap)
    loop(1, 16, lambda t: sent(g_send(t)))
    loop(1, 8, lambda t: sent(gz_send(t)))
    loop(1, 16, lambda t: sent(ga_send(t)))
    sent(g_forward)
    sent(w_swap)
    loop(1, 16, lambda t: sent(w_send(t)))
    loop(1, 16, lambda t: sent(wa_send(t)))
    loop(0, 4, lambda g: sent(wf(c, g)))
    loop(1, 8, lambda t: sent(nz_send(t)))


W_SUM_AT, W_FORWARD_AT = 1, 3


def per_device(momentum, gradient, right_factor):
    f32 = jnp.float32
    vmem, sem = pltpu.VMEM, pltpu.SemaphoreType.DMA
    scratch = [
        vmem((ROWS, COLS), f32), vmem((ROWS, COLS), jnp.bfloat16), vmem((ROWS, COLS), f32),
        vmem((4, 4, 2, 16, COLS), f32), vmem((4, ROWS, BLOCK), f32), vmem((8, 4, STRIP, BLOCK), f32),
        vmem((8, 4, STRIP, BLOCK), f32),
        vmem((16, 2, STRIP, BLOCK), f32), vmem((16, STRIP, BLOCK), f32), vmem((16, STRIP, BLOCK), f32),
        vmem((16, STRIP, BLOCK), f32), vmem((8, STRIP, BLOCK), f32), vmem((16, 2, STRIP, BLOCK), f32),
        vmem((RANK, RANK), f32),
        vmem((16, 2, 16, COLS), f32), vmem((16, 16, COLS), f32), vmem((16, 16, COLS), f32),
        vmem((16, 16, COLS), f32), vmem((16, 2, 16, COLS), f32), vmem((32, 16, COLS), f32),
        vmem((ROWS, RANK), f32), vmem((ROWS, RANK), f32), vmem((8, 8, RANK), f32), vmem((32, 16, BLOCK), f32),
        sem((3,)), sem((16,)), sem((16,)), sem((4,)), sem((4,)), sem((4, 8)), sem((4, 8)), sem((8,)), sem((8,)),
        sem((1,)), sem((1,)), sem((16,)), sem((16,)), sem((8,)), sem((8,)), sem((16,)), sem((16,)),
        sem((1,)), sem((1,)),
        sem((1,)), sem((1,)), sem((16,)), sem((16,)), sem((16,)), sem((16,)), sem((4,)), sem((4,)),
        sem((8,)), sem((8,)),
    ]
    return pl.pallas_call(
        step_kernel,
        out_shape=(
            jax.ShapeDtypeStruct((ROWS, COLS), f32),
            jax.ShapeDtypeStruct((16, COLS), f32),
            jax.ShapeDtypeStruct((ROWS, COLS), jnp.bfloat16),
        ),
        in_specs=[pl.BlockSpec(memory_space=pl.ANY)] * 3,
        out_specs=[pl.BlockSpec(memory_space=pltpu.VMEM)] * 3,
        scratch_shapes=scratch,
        compiler_params=pltpu.CompilerParams(
            collective_id=0, has_side_effects=True, vmem_limit_bytes=48 << 20
        ),
    )(momentum, gradient, right_factor)


def solution(mesh):
    finer = Mesh(
        mesh.devices.reshape(4, 4, 2, mesh.shape["narrow"]),
        ("wide_0", "wide_1", "wide_2", "narrow"),
    )
    return jax.shard_map(
        per_device,
        mesh=finer,
        in_specs=(P(WIDE, "narrow"), P(WIDE, "narrow"), P(WIDE, "narrow")),
        out_specs=(P(WIDE, "narrow"), P(WIDE, "narrow"), P(WIDE, "narrow")),
        check_vma=False,
    )
```

```python
import functools
import jax
import jax.numpy as jnp
from jax import lax
from jax.experimental import pallas as pl
from jax.experimental.pallas import tpu as pltpu
from jax.sharding import Mesh
from jax.sharding import PartitionSpec as P

N_COLS = 9216
WIDE = ("wide_0", "wide_1", "wide_2")
EPS = 1e-06
MU = 0.95
MESH = pl.DeviceIdType.MESH
ROWS, COLS, RANK, STRIP, BLOCK = 288, 1152, 512, 40, 128
PAIRS = [(i, j) for i in range(4) for j in range(i + 1)]


def product(a, b, ca, cb):
    return lax.dot_general(a, b, (((ca,), (cb,)), ((), ())), preferred_element_type=jnp.float32)


def split(v):
    high = v.astype(jnp.bfloat16)
    return high, (v - high.astype(jnp.float32)).astype(jnp.bfloat16)


def dot_split(a, b, ca, cb):
    small = product(a[0], b[1], ca, cb) + product(a[1], b[0], ca, cb)
    return product(a[0], b[0], ca, cb) + small


def dot(a, b, ca, cb):
    return dot_split(split(a), split(b), ca, cb)


def dot_nt(a, b):
    return dot(a, b, 1, 1)


def dot_nn(a, b):
    return dot(a, b, 1, 0)


def lane_of(tile, lane):
    return jnp.broadcast_to(tile[:, lane:lane + 1], tile.shape)

def row_of(tile, row):
    return jnp.broadcast_to(tile[row:row + 1, :], tile.shape)

def inv_chol_block(d, hook):
    n = 128
    tiles = [d[8 * i:8 * i + 8, :] for i in range(n // 8)]
    lanes = lax.broadcasted_iota(jnp.int32, (8, n), 1)
    subs = lax.broadcasted_iota(jnp.int32, (8, n), 0)
    for j in range(n // 8):
        hook(j)
        t = tiles[j]
        inside = (lanes >= 8 * j) & (lanes < 8 * j + 8)
        cols = [lane_of(t, 8 * j + k) for k in range(8)]
        e = {(i, k): row_of(cols[k], i) for k in range(8) for i in range(k, 8)}
        raw = {i: [lane_of(tiles[i], 8 * j + k) for k in range(8)] for i in range(j + 1, n // 8)}
        own = jnp.where(inside, jnp.where(lanes - 8 * j == subs, 1.0, 0.0), t)
        rows = [row_of(own, k) for k in range(8)]
        scale, low = [], {}
        for k in range(8):
            scale.append(lax.rsqrt(e[k, k]))
            for i in range(k + 1, 8):
                low[i, k] = e[i, k] * scale[k]
            for i in range(k + 1, 8):
                for m in range(k + 1, i + 1):
                    e[i, m] = e[i, m] - low[i, k] * low[m, k]
        def forward(values):
            out = []
            for k in range(8):
                v = values[k]
                for m in range(k):
                    v = v - low[k, m] * out[m]
                out.append(v * scale[k])
            return out
        up = forward(rows)
        new = up[0]
        for k in range(1, 8):
            new = jnp.where(subs == k, up[k], new)
        tiles[j] = new
        for i in range(j + 1, n // 8):
            c = forward(raw[i])
            v = jnp.where(inside, 0.0, tiles[i])
            for k in range(8):
                v = v - c[k] * up[k]
            tiles[i] = v
    x = jnp.concatenate(tiles, axis=0)
    r = lax.broadcasted_iota(jnp.int32, (n, n), 0)
    c = lax.broadcasted_iota(jnp.int32, (n, n), 1)
    return jnp.where(c <= r, x, 0.0)

def inv_chol(m_ref, hooks, nb=4):
    b = 128
    for k in range(nb):
        s = slice(b * k, b * k + b)
        x = inv_chol_block(m_ref[s, s], lambda j: hooks.get((k, j), lambda: None)())
        if k:
            left = m_ref[s, :b * k]
            left = dot_nn(x, left)
            m_ref[s, :b * k] = left
        m_ref[s, s] = x
        for i in range(k + 1, nb):
            t = slice(b * i, b * i + b)
            c = dot_nt(m_ref[t, s], x)
            m_ref[t, s] = c
        for i in range(k + 1, nb):
            t = slice(b * i, b * i + b)
            c = m_ref[t, s]
            for q in range(k + 1, i + 1):
                u = slice(b * q, b * q + b)
                m_ref[t, u] = m_ref[t, u] - dot_nt(c, m_ref[u, s])
        for i in range(nb - 1, k, -1):
            t = slice(b * i, b * i + b)
            c = m_ref[t, s]
            if k:
                m_ref[t, :b * k] = m_ref[t, :b * k] - dot_nn(c, m_ref[s, :b * k])
            m_ref[t, s] = -dot_nn(c, x)
    for k in range(nb):
        for q in range(k + 1, nb):
            m_ref[b * k:b * k + b, b * q:b * q + b] = jnp.zeros((b, b), jnp.float32)


def step_kernel(
    momentum, gradient, right, new_momentum, new_right, update,
    mom, grad, a, a_h, a_l, r_all, part, z_got, p_all, g_part, g_comb, g_half, g_got, g_z, g_all, m,
    w_part, w_comb, w_half, w_got, w_all, s, p, q, n_z, roots,
    local, r_s, r_r, rf_s, rf_r, z_s, z_r, p_s, p_r, gc_s, gc_r, gr_s, gr_r, gz_s, gz_r, ga_s, ga_r, gf_s, gf_r,
    wc_s, wc_r, wr_s, wr_r, wa_s, wa_r, wf_s, wf_r, nz_s, nz_r,
):
    x, y, c, z = (lax.axis_index(n) for n in (*WIDE, "narrow"))
    xy = x * 4 + y
    sibling = (x, y, 1 - c, z)

    def plane(t):
        return (lax.rem(x + t // 4, 4), lax.rem(y + lax.rem(t, 4), 4), c, z)

    def plane_from(t):
        return lax.rem(x + 4 - t // 4, 4) * 4 + lax.rem(y + 4 - lax.rem(t, 4), 4)

    def column(t):
        return (x, y, c, lax.rem(z + t, 8))

    def column_from(t):
        return lax.rem(z + 8 - t, 8)

    def remote(src, dst, send, recv, to):
        return pltpu.make_async_remote_copy(
            src_ref=src, dst_ref=dst, send_sem=send, recv_sem=recv, device_id=to, device_id_type=MESH
        )

    pending = []

    def start_all(low, high, make):
        loop(low, high, lambda t: make(t).start())
        pending.append((low, high, make))

    def finish():
        for low, high, make in pending:
            loop(low, high, lambda t: make(t).wait_send())

    def loop(low, high, body):
        def run(i, carry):
            body(i)
            return carry

        lax.fori_loop(low, high, run, 0)

    loads = [
        pltpu.make_async_copy(right, r_all.at[x, y, c], local.at[0]),
        pltpu.make_async_copy(momentum, mom, local.at[1]),
        pltpu.make_async_copy(gradient, grad, local.at[2]),
    ]
    for load in loads:
        load.start()

    barrier = pltpu.get_barrier_semaphore()

    def hello(to):
        pl.semaphore_signal(barrier, inc=1, device_id=to, device_id_type=MESH)

    hello(sibling)
    loop(1, 16, lambda t: hello(plane(t)))
    loop(1, 8, lambda t: hello(column(t)))
    pl.semaphore_wait(barrier, 23)

    sense = 1 - 2 * c

    def wrap4(v):
        return lax.rem(v + 4, 4)

    def wrap8(v):
        return lax.rem(v + 8, 8)

    class PlaneGather:
        def __init__(self, piece, send, recv):
            self.piece, self.send, self.recv = piece, send, recv
            self.here = ((x, y), (y, x))

        def ref(self, h, u, v):
            return self.piece(h, u, v) if h == 0 else self.piece(h, v, u)

        def device(self, h, u, v):
            return (u, v, c, z) if h == 0 else (v, u, c, z)

        def go(self, h, index, origin, to):
            u, v = origin
            block = self.ref(h, wrap4(u), wrap4(v))
            i = 15 * h + index
            start_all(0, 1, lambda t: remote(
                block, block, self.send.at[i], self.recv.at[i], self.device(h, wrap4(to[0]), wrap4(to[1]))
            ))

        def come(self, h, index, origin):
            u, v = origin
            block = self.ref(h, wrap4(u), wrap4(v))
            i = 15 * h + index
            remote(block, block, self.send.at[i], self.recv.at[i], sibling).wait_recv()

        def origin(self, h, k):
            return self.here[h][0] + (0, -1, 1, 2)[k]

        def second(self, h, k):
            u0, v0 = self.here[h]
            u = self.origin(h, k)
            for j, hop in enumerate((2, 1, -1)):
                self.go(h, 3 + 3 * k + j, (u, v0), (u0, v0 + hop))

        def second_end(self, h, k):
            u, v0 = self.origin(h, k), self.here[h][1]
            for j, hop in enumerate((2, 1, -1)):
                self.come(h, 3 + 3 * k + j, (u, v0 - hop))

        def first(self):
            for j, hop in enumerate((2, 1, -1)):
                for h in range(2):
                    u0, v0 = self.here[h]
                    self.go(h, j, (u0, v0), (u0 + hop, v0))
            for h in range(2):
                self.second(h, 0)

        def middle(self):
            for k, j in ((1, 1), (2, 2), (3, 0)):
                for h in range(2):
                    self.come(h, j, (self.origin(h, k), self.here[h][1]))
                    self.second(h, k)

        def last(self, k):
            for h in range(2):
                self.second_end(h, k)

    def half_rows(h):
        return pl.ds(8 * h, 8)

    gather = PlaneGather(lambda h, xi, yi: r_all.at[xi, yi, c, half_rows(h)], r_s, r_r)

    def r_column(h, k, v):
        u = wrap4(gather.origin(h, k))
        return r_all.at[u, :, v, half_rows(h)] if h == 0 else r_all.at[:, u, v, half_rows(h)]

    def r_forward(h, k, v):
        block = r_column(h, k, v)
        return remote(block, block, rf_s.at[4 * h + k], rf_r.at[4 * h + k], sibling)

    def r_share(k):
        for h in range(2):
            start_all(0, 1, lambda t, h=h: r_forward(h, k, c))

    loads[0].wait()
    gather.first()
    loads[1].wait()
    loads[2].wait()
    a[...] = mom[...] + grad[...].astype(jnp.float32)
    a_h[...], a_l[...] = split(a[...])
    gather.middle()
    for k in range(4):
        gather.last(k)
        r_share(k)

    def z_rows(t):
        return pl.ds(pl.multiple_of(8 * ((9 * t) // 2), 8), STRIP)

    def z_target(d, n):
        return wrap8(z + (sense * (4 - n) if d == 0 else -sense * (3 - n)))

    def z_send(d, n, g):
        to = (x, y, c, wrap8(z + (sense if d == 0 else -sense)))
        src = part.at[g, z_rows(z_target(d, 0))] if n == 0 else z_got.at[d, n - 1, g]
        return remote(src, z_got.at[d, n, g], z_s.at[d, n, g], z_r.at[d, n, g], to)

    def z_wait(d, n, g):
        block = z_got.at[d, n, g]
        remote(block, block, z_s.at[d, n, g], z_r.at[d, n, g], sibling).wait_recv()

    for k in range(4):
        for h in range(2):
            r_forward(h, k, 1 - c).wait_recv()
    for g in range(4):
        ranks = split(r_all[g].reshape(BLOCK, COLS))
        part[g] = dot_split((a_h[...], a_l[...]), ranks, 1, 1)
        for d in range(2):
            start_all(0, 1, lambda t, d=d, g=g: z_send(d, 0, g))
    for n in range(1, 4):
        for g in range(4):
            for d in range(2):
                if d == 0 or n < 3:
                    z_wait(d, n - 1, g)
                    z_got[d, n - 1, g] = z_got[d, n - 1, g] + part[g, z_rows(z_target(d, n))]
                    start_all(0, 1, lambda t, d=d, n=n, g=g: z_send(d, n, g))
    total = []
    for g in range(4):
        z_wait(1, 2, g)
        z_wait(0, 3, g)
        total.append(part[g, z_rows(z)] + (z_got[0, 3, g] + z_got[1, 2, g]))
    for g in range(4):
        p_all[pl.ds(z, 1), g] = total[g].reshape(1, STRIP, BLOCK)

    def p_send(d, n, e):
        to = (x, y, c, wrap8(z + (sense if d == 0 else -sense)))
        block = p_all.at[wrap8(z - n * sense if d == 0 else z + n * sense), 2 * e : 2 * e + 2]
        return remote(block, block, p_s.at[d, n, e], p_r.at[d, n, e], to)

    def p_wait(d, n, e):
        block = p_all.at[wrap8(z - (n + 1) * sense if d == 0 else z + (n + 1) * sense), 2 * e : 2 * e + 2]
        remote(block, block, p_s.at[d, n, e], p_r.at[d, n, e], sibling).wait_recv()

    def p_step(n):
        for e in range(2):
            for d in range(2):
                if n > 0 and (d == 0 or n < 4):
                    p_wait(d, n - 1, e)
                if n < (4, 3)[d]:
                    start_all(0, 1, lambda t, d=d, e=e: p_send(d, n, e))

    p_step(0)

    tile_rows = lax.broadcasted_iota(jnp.int32, (STRIP, BLOCK), 0)
    fresh = (tile_rows >= 8) | (lax.rem(z, 2) == 0)
    own = [jnp.where(fresh, total[i], 0.0) for i in range(4)]
    pieces = []
    for i in range(4):
        wide = jnp.concatenate(own[: i + 1], axis=1)
        strip = dot(own[i], wide, 0, 0)
        pieces += [strip[:, BLOCK * j : BLOCK * j + BLOCK] for j in range(i + 1)]
    g_part[...] = jnp.concatenate(pieces, axis=0).reshape(16, 2, STRIP, BLOCK)

    p_step(1)
    g_swap = remote(g_part.at[:, 1 - c], g_comb, gc_s.at[0], gc_r.at[0], sibling)
    start_all(0, 1, lambda t: g_swap)
    g_swap.wait_recv()
    g_half[...] = g_part[:, pl.ds(c, 1)].reshape(16, STRIP, BLOCK) + g_comb[...]

    def g_send(t):
        tx, ty, _, _ = plane(t)
        return remote(g_half.at[tx * 4 + ty], g_got.at[t], gr_s.at[t], gr_r.at[t], plane(t))

    def g_wait(t):
        remote(g_got.at[t], g_got.at[t], gr_s.at[t], gr_r.at[t], plane(t)).wait_recv()

    start_all(1, 16, g_send)
    p_step(2)
    p_step(3)
    loop(1, 16, g_wait)
    strip = g_half[pl.ds(xy, 1)].reshape(STRIP, BLOCK)
    for t in range(1, 16):
        strip = strip + g_got[t]
    g_z[pl.ds(z, 1)] = strip.reshape(1, STRIP, BLOCK)

    def gz_send(t):
        return remote(g_z.at[z], g_z.at[z], gz_s.at[t], gz_r.at[t], column(t))

    def gz_wait(t):
        f = column_from(t)
        remote(g_z.at[f], g_z.at[f], gz_s.at[t], gz_r.at[t], column(t)).wait_recv()

    start_all(1, 8, gz_send)
    p_step(4)
    for t in range(8):
        first = (9 * t) // 2
        skip = t % 2
        for i in range(4):
            p[8 * (first + skip) : 8 * (first + 5), BLOCK * i : BLOCK * i + BLOCK] = p_all[t, i, 8 * skip :]
    for i in range(4):
        lanes = slice(BLOCK * i, BLOCK * i + BLOCK)
        w_part[4 * i : 4 * i + 4] = dot_split(split(p[:, lanes]), (a_h[...], a_l[...]), 0, 0).reshape(4, 2, 16, COLS)
    w_swap = remote(w_part.at[:, 1 - c], w_comb, wc_s.at[0], wc_r.at[0], sibling)
    start_all(0, 1, lambda t: w_swap)

    loop(1, 8, gz_wait)
    strip = g_z[0]
    for t in range(1, 8):
        strip = strip + g_z[t]
    g_all[pl.ds(xy, 1), pl.ds(c, 1)] = strip.reshape(1, 1, STRIP, BLOCK)

    def ga_send(t):
        return remote(g_all.at[xy, c], g_all.at[xy, c], ga_s.at[t], ga_r.at[t], plane(t))

    def ga_wait(t):
        f = plane_from(t)
        remote(g_all.at[f, c], g_all.at[f, c], ga_s.at[t], ga_r.at[t], plane(t)).wait_recv()

    start_all(1, 16, ga_send)

    w_swap.wait_recv()
    w_half[...] = w_part[:, pl.ds(c, 1)].reshape(16, 16, COLS) + w_comb[...]

    def w_send(t):
        tx, ty, _, _ = plane(t)
        return remote(w_half.at[tx * 4 + ty], w_got.at[t], wr_s.at[t], wr_r.at[t], plane(t))

    def w_wait(t):
        remote(w_got.at[t], w_got.at[t], wr_s.at[t], wr_r.at[t], plane(t)).wait_recv()

    start_all(1, 16, w_send)
    loop(1, 16, ga_wait)
    g_forward = remote(g_all.at[:, c], g_all.at[:, c], gf_s.at[0], gf_r.at[0], sibling)
    start_all(0, 1, lambda t: g_forward)

    remote(g_all.at[:, 1 - c], g_all.at[:, 1 - c], gf_s.at[0], gf_r.at[0], sibling).wait_recv()
    for n, (i, j) in enumerate(PAIRS):
        for k in range(16):
            t = 16 * n + k
            o, e = divmod(t, 5)
            m[BLOCK * i + 8 * k : BLOCK * i + 8 * k + 8, BLOCK * j : BLOCK * j + BLOCK] = g_all[
                o // 2, o % 2, 8 * e : 8 * e + 8
            ]

    w_gather = PlaneGather(lambda h, xi, yi: w_all.at[xi, yi, c, half_rows(h)], wa_s, wa_r)

    def w_own():
        loop(1, 16, w_wait)
        own = w_half[pl.ds(xy, 1)].reshape(16, COLS)
        for t in range(1, 16):
            own = own + w_got[t]
        w_all[pl.ds(x, 1), pl.ds(y, 1), pl.ds(c, 1)] = own.reshape(1, 1, 1, 16, COLS)

    def w_column(h, k, v):
        u = wrap4(w_gather.origin(h, k))
        block = w_all.at[u, :, v, half_rows(h)] if h == 0 else w_all.at[:, u, v, half_rows(h)]
        return remote(block, block, wf_s.at[4 * h + k], wf_r.at[4 * h + k], sibling)

    def w_share():
        for k in range(4):
            w_gather.last(k)
            for h in range(2):
                start_all(0, 1, lambda t, h=h, k=k: w_column(h, k, c))

    def w_first():
        w_own()
        w_gather.first()

    hooks = {WHEN[0]: w_first, WHEN[1]: w_gather.middle, WHEN[2]: w_share}
    inv_chol(m, hooks)

    for i in range(4):
        lanes = slice(BLOCK * i, BLOCK * i + BLOCK)
        q[:, lanes] = dot(p[:, : BLOCK * i + BLOCK], m[lanes, : BLOCK * i + BLOCK], 1, 1)
    for k in range(4):
        for h in range(2):
            w_column(h, k, 1 - c).wait_recv()
    squares = jnp.zeros((8, RANK), jnp.float32)
    ones = jnp.ones((8, COLS), jnp.float32)
    for i in range(4):
        rows = slice(BLOCK * i, BLOCK * i + BLOCK)
        known = w_all[: i + 1].reshape(BLOCK * i + BLOCK, COLS)
        block = dot(m[rows, : BLOCK * i + BLOCK], known, 1, 0)
        s[8 * i : 8 * i + 8] = block.reshape(8, 16, COLS)
        n_z[pl.ds(z, 1), :, rows] = dot(ones, block * block, 1, 1).reshape(1, 8, BLOCK)

    def nz_send(t):
        return remote(n_z.at[z], n_z.at[z], nz_s.at[t], nz_r.at[t], column(t))

    def nz_wait(t):
        f = column_from(t)
        remote(n_z.at[f], n_z.at[f], nz_s.at[t], nz_r.at[t], column(t)).wait_recv()

    start_all(1, 8, nz_send)
    sums = s[...].reshape(RANK, COLS)
    new_momentum[...] = a[...] - (1.0 - MU) * dot(q[...], sums, 1, 0)
    loop(1, 8, nz_wait)
    squares = n_z[0]
    for t in range(1, 8):
        squares = squares + n_z[t]
    root = jnp.sqrt(squares / N_COLS + EPS)
    update[...] = dot(q[...] * (1.0 / root[:1]), sums, 1, 0).astype(jnp.bfloat16)
    for i in range(4):
        turned = jnp.broadcast_to(root[:1, BLOCK * i : BLOCK * i + BLOCK], (BLOCK, BLOCK)).T
        roots[8 * i : 8 * i + 8] = turned.reshape(8, 16, BLOCK)
    mine = xy * 2 + c
    scale = roots[pl.ds(mine, 1)].reshape(16, BLOCK)
    strip = s[pl.ds(mine, 1)].reshape(16, COLS)
    for k in range(9):
        new_right[:, BLOCK * k : BLOCK * k + BLOCK] = strip[:, BLOCK * k : BLOCK * k + BLOCK] / scale

    finish()


WHEN = ((1, 4), (2, 4), (3, 6))


def per_device(momentum, gradient, right_factor):
    f32 = jnp.float32
    vmem, sem = pltpu.VMEM, pltpu.SemaphoreType.DMA
    scratch = [
        vmem((ROWS, COLS), f32), vmem((ROWS, COLS), jnp.bfloat16), vmem((ROWS, COLS), f32),
        vmem((ROWS, COLS), jnp.bfloat16), vmem((ROWS, COLS), jnp.bfloat16),
        vmem((4, 4, 2, 16, COLS), f32), vmem((4, ROWS, BLOCK), f32), vmem((2, 4, 4, STRIP, BLOCK), f32),
        vmem((8, 4, STRIP, BLOCK), f32),
        vmem((16, 2, STRIP, BLOCK), f32), vmem((16, STRIP, BLOCK), f32), vmem((16, STRIP, BLOCK), f32),
        vmem((16, STRIP, BLOCK), f32), vmem((8, STRIP, BLOCK), f32), vmem((16, 2, STRIP, BLOCK), f32),
        vmem((RANK, RANK), f32),
        vmem((16, 2, 16, COLS), f32), vmem((16, 16, COLS), f32), vmem((16, 16, COLS), f32),
        vmem((16, 16, COLS), f32), vmem((4, 4, 2, 16, COLS), f32),
        vmem((32, 16, COLS), f32),
        vmem((ROWS, RANK), f32), vmem((ROWS, RANK), f32), vmem((8, 8, RANK), f32), vmem((32, 16, BLOCK), f32),
        sem((3,)), sem((30,)), sem((30,)), sem((8,)), sem((8,)), sem((2, 4, 4)), sem((2, 4, 4)),
        sem((2, 4, 2)), sem((2, 4, 2)),
        sem((1,)), sem((1,)), sem((16,)), sem((16,)), sem((8,)), sem((8,)), sem((16,)), sem((16,)),
        sem((1,)), sem((1,)),
        sem((1,)), sem((1,)), sem((16,)), sem((16,)), sem((30,)), sem((30,)), sem((8,)), sem((8,)),
        sem((8,)), sem((8,)),
    ]
    return pl.pallas_call(
        step_kernel,
        out_shape=(
            jax.ShapeDtypeStruct((ROWS, COLS), f32),
            jax.ShapeDtypeStruct((16, COLS), f32),
            jax.ShapeDtypeStruct((ROWS, COLS), jnp.bfloat16),
        ),
        in_specs=[pl.BlockSpec(memory_space=pl.ANY)] * 3,
        out_specs=[pl.BlockSpec(memory_space=pltpu.VMEM)] * 3,
        scratch_shapes=scratch,
        compiler_params=pltpu.CompilerParams(
            collective_id=0, has_side_effects=True, vmem_limit_bytes=60 << 20
        ),
    )(momentum, gradient, right_factor)


def solution(mesh):
    finer = Mesh(
        mesh.devices.reshape(4, 4, 2, mesh.shape["narrow"]),
        ("wide_0", "wide_1", "wide_2", "narrow"),
    )
    return jax.shard_map(
        per_device,
        mesh=finer,
        in_specs=(P(WIDE, "narrow"), P(WIDE, "narrow"), P(WIDE, "narrow")),
        out_specs=(P(WIDE, "narrow"), P(WIDE, "narrow"), P(WIDE, "narrow")),
        check_vma=False,
    )
```

```python
import functools
import jax
import jax.numpy as jnp
from jax import lax
from jax.experimental import pallas as pl
from jax.experimental.pallas import tpu as pltpu
from jax.sharding import Mesh
from jax.sharding import PartitionSpec as P

N_COLS = 9216
WIDE = ("wide_0", "wide_1", "wide_2")
EPS = 1e-06
MU = 0.95
MESH = pl.DeviceIdType.MESH
ROWS, COLS, RANK, STRIP, BLOCK = 288, 1152, 512, 40, 128
PAIRS = [(i, j) for i in range(4) for j in range(i + 1)]


def product(a, b, ca, cb):
    return lax.dot_general(a, b, (((ca,), (cb,)), ((), ())), preferred_element_type=jnp.float32)


def split(v):
    high = v.astype(jnp.bfloat16)
    return high, (v - high.astype(jnp.float32)).astype(jnp.bfloat16)


def dot_split(a, b, ca, cb):
    small = product(a[0], b[1], ca, cb) + product(a[1], b[0], ca, cb)
    return product(a[0], b[0], ca, cb) + small


def dot(a, b, ca, cb):
    return dot_split(split(a), split(b), ca, cb)


def dot_nt(a, b):
    return dot(a, b, 1, 1)


def dot_nn(a, b):
    return dot(a, b, 1, 0)


def lane_of(tile, lane):
    return jnp.broadcast_to(tile[:, lane:lane + 1], tile.shape)

def row_of(tile, row):
    return jnp.broadcast_to(tile[row:row + 1, :], tile.shape)

def inv_chol_block(d, hook):
    n = 128
    tiles = [d[8 * i:8 * i + 8, :] for i in range(n // 8)]
    lanes = lax.broadcasted_iota(jnp.int32, (8, n), 1)
    subs = lax.broadcasted_iota(jnp.int32, (8, n), 0)
    for j in range(n // 8):
        hook(j)
        t = tiles[j]
        inside = (lanes >= 8 * j) & (lanes < 8 * j + 8)
        cols = [lane_of(t, 8 * j + k) for k in range(8)]
        e = {(i, k): row_of(cols[k], i) for k in range(8) for i in range(k, 8)}
        raw = {i: [lane_of(tiles[i], 8 * j + k) for k in range(8)] for i in range(j + 1, n // 8)}
        own = jnp.where(inside, jnp.where(lanes - 8 * j == subs, 1.0, 0.0), t)
        rows = [row_of(own, k) for k in range(8)]
        scale, low = [], {}
        for k in range(8):
            scale.append(lax.rsqrt(e[k, k]))
            for i in range(k + 1, 8):
                low[i, k] = e[i, k] * scale[k]
            for i in range(k + 1, 8):
                for m in range(k + 1, i + 1):
                    e[i, m] = e[i, m] - low[i, k] * low[m, k]
        def forward(values):
            out = []
            for k in range(8):
                v = values[k]
                for m in range(k):
                    v = v - low[k, m] * out[m]
                out.append(v * scale[k])
            return out
        up = forward(rows)
        new = up[0]
        for k in range(1, 8):
            new = jnp.where(subs == k, up[k], new)
        tiles[j] = new
        for i in range(j + 1, n // 8):
            c = forward(raw[i])
            v = jnp.where(inside, 0.0, tiles[i])
            for k in range(8):
                v = v - c[k] * up[k]
            tiles[i] = v
    x = jnp.concatenate(tiles, axis=0)
    r = lax.broadcasted_iota(jnp.int32, (n, n), 0)
    c = lax.broadcasted_iota(jnp.int32, (n, n), 1)
    return jnp.where(c <= r, x, 0.0)

def inv_chol(m_ref, hooks, nb=4):
    b = 128
    for k in range(nb):
        s = slice(b * k, b * k + b)
        x = inv_chol_block(m_ref[s, s], lambda j: hooks.get((k, j), lambda: None)())
        if k:
            left = m_ref[s, :b * k]
            left = dot_nn(x, left)
            m_ref[s, :b * k] = left
        m_ref[s, s] = x
        for i in range(k + 1, nb):
            t = slice(b * i, b * i + b)
            c = dot_nt(m_ref[t, s], x)
            m_ref[t, s] = c
        for i in range(k + 1, nb):
            t = slice(b * i, b * i + b)
            c = m_ref[t, s]
            for q in range(k + 1, i + 1):
                u = slice(b * q, b * q + b)
                m_ref[t, u] = m_ref[t, u] - dot_nt(c, m_ref[u, s])
        for i in range(nb - 1, k, -1):
            t = slice(b * i, b * i + b)
            c = m_ref[t, s]
            if k:
                m_ref[t, :b * k] = m_ref[t, :b * k] - dot_nn(c, m_ref[s, :b * k])
            m_ref[t, s] = -dot_nn(c, x)
    for k in range(nb):
        for q in range(k + 1, nb):
            m_ref[b * k:b * k + b, b * q:b * q + b] = jnp.zeros((b, b), jnp.float32)


def step_kernel(
    momentum, gradient, right, new_momentum, new_right, update,
    mom, grad, a, a_h, a_l, r_all, part, z_got, p_all, g_part, g_comb, g_half, g_got, g_z, g_all, m,
    w_part, w_comb, w_half, w_got, w_h, w_l, w_all, s, p, q, n_z, roots,
    local, r_s, r_r, rf_s, rf_r, z_s, z_r, p_s, p_r, gc_s, gc_r, gr_s, gr_r, gz_s, gz_r, ga_s, ga_r, gf_s, gf_r,
    wc_s, wc_r, wr_s, wr_r, wa_s, wa_r, wf_s, wf_r, nz_s, nz_r,
):
    x, y, c, z = (lax.axis_index(n) for n in (*WIDE, "narrow"))
    xy = x * 4 + y
    sibling = (x, y, 1 - c, z)

    def plane(t):
        return (lax.rem(x + t // 4, 4), lax.rem(y + lax.rem(t, 4), 4), c, z)

    def plane_from(t):
        return lax.rem(x + 4 - t // 4, 4) * 4 + lax.rem(y + 4 - lax.rem(t, 4), 4)

    def column(t):
        return (x, y, c, lax.rem(z + t, 8))

    def column_from(t):
        return lax.rem(z + 8 - t, 8)

    def remote(src, dst, send, recv, to):
        return pltpu.make_async_remote_copy(
            src_ref=src, dst_ref=dst, send_sem=send, recv_sem=recv, device_id=to, device_id_type=MESH
        )

    pending = []

    def start_all(low, high, make):
        loop(low, high, lambda t: make(t).start())
        pending.append((low, high, make))

    def finish():
        for low, high, make in pending:
            loop(low, high, lambda t: make(t).wait_send())

    def loop(low, high, body):
        def run(i, carry):
            body(i)
            return carry

        lax.fori_loop(low, high, run, 0)

    loads = [
        pltpu.make_async_copy(right, r_all.at[x, y, c], local.at[0]),
        pltpu.make_async_copy(momentum, mom, local.at[1]),
        pltpu.make_async_copy(gradient, grad, local.at[2]),
    ]
    for load in loads:
        load.start()

    barrier = pltpu.get_barrier_semaphore()

    def hello(to):
        pl.semaphore_signal(barrier, inc=1, device_id=to, device_id_type=MESH)

    hello(sibling)
    loop(1, 16, lambda t: hello(plane(t)))
    loop(1, 8, lambda t: hello(column(t)))
    pl.semaphore_wait(barrier, 23)

    sense = 1 - 2 * c

    def wrap4(v):
        return lax.rem(v + 4, 4)

    def wrap8(v):
        return lax.rem(v + 8, 8)

    class PlaneGather:
        def __init__(self, piece, send, recv):
            self.piece, self.send, self.recv = piece, send, recv
            self.here = ((x, y), (y, x))

        def ref(self, h, u, v):
            return self.piece(h, u, v) if h == 0 else self.piece(h, v, u)

        def device(self, h, u, v):
            return (u, v, c, z) if h == 0 else (v, u, c, z)

        def go(self, h, index, origin, to):
            u, v = origin
            block = self.ref(h, wrap4(u), wrap4(v))
            i = 15 * h + index
            start_all(0, 1, lambda t: remote(
                block, block, self.send.at[i], self.recv.at[i], self.device(h, wrap4(to[0]), wrap4(to[1]))
            ))

        def come(self, h, index, origin):
            u, v = origin
            block = self.ref(h, wrap4(u), wrap4(v))
            i = 15 * h + index
            remote(block, block, self.send.at[i], self.recv.at[i], sibling).wait_recv()

        def origin(self, h, k):
            return self.here[h][0] + (0, -1, 1, 2)[k]

        def second(self, h, k):
            u0, v0 = self.here[h]
            u = self.origin(h, k)
            for j, hop in enumerate((2, 1, -1)):
                self.go(h, 3 + 3 * k + j, (u, v0), (u0, v0 + hop))

        def second_end(self, h, k):
            u, v0 = self.origin(h, k), self.here[h][1]
            for j, hop in enumerate((2, 1, -1)):
                self.come(h, 3 + 3 * k + j, (u, v0 - hop))

        def first(self):
            for j, hop in enumerate((2, 1, -1)):
                for h in range(2):
                    u0, v0 = self.here[h]
                    self.go(h, j, (u0, v0), (u0 + hop, v0))
            for h in range(2):
                self.second(h, 0)

        def middle(self):
            for k, j in ((1, 1), (2, 2), (3, 0)):
                for h in range(2):
                    self.come(h, j, (self.origin(h, k), self.here[h][1]))
                    self.second(h, k)

        def last(self, k):
            for h in range(2):
                self.second_end(h, k)

    def half_rows(h):
        return pl.ds(8 * h, 8)

    gather = PlaneGather(lambda h, xi, yi: r_all.at[xi, yi, c, half_rows(h)], r_s, r_r)

    def r_column(h, k, v):
        u = wrap4(gather.origin(h, k))
        return r_all.at[u, :, v, half_rows(h)] if h == 0 else r_all.at[:, u, v, half_rows(h)]

    def r_forward(h, k, v):
        block = r_column(h, k, v)
        return remote(block, block, rf_s.at[4 * h + k], rf_r.at[4 * h + k], sibling)

    def r_share(k):
        for h in range(2):
            start_all(0, 1, lambda t, h=h: r_forward(h, k, c))

    loads[0].wait()
    gather.first()
    loads[1].wait()
    loads[2].wait()
    a[...] = mom[...] + grad[...].astype(jnp.float32)
    a_h[...], a_l[...] = split(a[...])
    gather.middle()
    for k in range(4):
        gather.last(k)
        r_share(k)

    def z_rows(t):
        return pl.ds(pl.multiple_of(8 * ((9 * t) // 2), 8), STRIP)

    def z_target(d, n):
        return wrap8(z + (sense * (4 - n) if d == 0 else -sense * (3 - n)))

    def z_send(d, n, g):
        to = (x, y, c, wrap8(z + (sense if d == 0 else -sense)))
        src = part.at[g, z_rows(z_target(d, 0))] if n == 0 else z_got.at[d, n - 1, g]
        return remote(src, z_got.at[d, n, g], z_s.at[d, n, g], z_r.at[d, n, g], to)

    def z_wait(d, n, g):
        block = z_got.at[d, n, g]
        remote(block, block, z_s.at[d, n, g], z_r.at[d, n, g], sibling).wait_recv()

    for k in range(4):
        for h in range(2):
            r_forward(h, k, 1 - c).wait_recv()
    for g in range(4):
        ranks = split(r_all[g].reshape(BLOCK, COLS))
        part[g] = dot_split((a_h[...], a_l[...]), ranks, 1, 1)
        for d in range(2):
            start_all(0, 1, lambda t, d=d, g=g: z_send(d, 0, g))
    for n in range(1, 4):
        for g in range(4):
            for d in range(2):
                if d == 0 or n < 3:
                    z_wait(d, n - 1, g)
                    z_got[d, n - 1, g] = z_got[d, n - 1, g] + part[g, z_rows(z_target(d, n))]
                    start_all(0, 1, lambda t, d=d, n=n, g=g: z_send(d, n, g))
    total = []
    for g in range(4):
        z_wait(1, 2, g)
        z_wait(0, 3, g)
        total.append(part[g, z_rows(z)] + (z_got[0, 3, g] + z_got[1, 2, g]))
    for g in range(4):
        p_all[pl.ds(z, 1), g] = total[g].reshape(1, STRIP, BLOCK)

    def p_send(d, n, e):
        to = (x, y, c, wrap8(z + (sense if d == 0 else -sense)))
        block = p_all.at[wrap8(z - n * sense if d == 0 else z + n * sense), 2 * e : 2 * e + 2]
        return remote(block, block, p_s.at[d, n, e], p_r.at[d, n, e], to)

    def p_wait(d, n, e):
        block = p_all.at[wrap8(z - (n + 1) * sense if d == 0 else z + (n + 1) * sense), 2 * e : 2 * e + 2]
        remote(block, block, p_s.at[d, n, e], p_r.at[d, n, e], sibling).wait_recv()

    def p_step(n):
        for e in range(2):
            for d in range(2):
                if n > 0 and (d == 0 or n < 4):
                    p_wait(d, n - 1, e)
                if n < (4, 3)[d]:
                    start_all(0, 1, lambda t, d=d, e=e: p_send(d, n, e))

    p_step(0)

    tile_rows = lax.broadcasted_iota(jnp.int32, (STRIP, BLOCK), 0)
    fresh = (tile_rows >= 8) | (lax.rem(z, 2) == 0)
    own = [jnp.where(fresh, total[i], 0.0) for i in range(4)]
    pieces = []
    for i in range(4):
        wide = jnp.concatenate(own[: i + 1], axis=1)
        strip = dot(own[i], wide, 0, 0)
        pieces += [strip[:, BLOCK * j : BLOCK * j + BLOCK] for j in range(i + 1)]
    g_part[...] = jnp.concatenate(pieces, axis=0).reshape(16, 2, STRIP, BLOCK)

    p_step(1)
    g_swap = remote(g_part.at[:, 1 - c], g_comb, gc_s.at[0], gc_r.at[0], sibling)
    start_all(0, 1, lambda t: g_swap)
    g_swap.wait_recv()
    g_half[...] = g_part[:, pl.ds(c, 1)].reshape(16, STRIP, BLOCK) + g_comb[...]

    def g_send(t):
        tx, ty, _, _ = plane(t)
        return remote(g_half.at[tx * 4 + ty], g_got.at[t], gr_s.at[t], gr_r.at[t], plane(t))

    def g_wait(t):
        remote(g_got.at[t], g_got.at[t], gr_s.at[t], gr_r.at[t], plane(t)).wait_recv()

    start_all(1, 16, g_send)
    p_step(2)
    p_step(3)
    loop(1, 16, g_wait)
    strip = g_half[pl.ds(xy, 1)].reshape(STRIP, BLOCK)
    for t in range(1, 16):
        strip = strip + g_got[t]
    g_z[pl.ds(z, 1)] = strip.reshape(1, STRIP, BLOCK)

    def gz_send(t):
        return remote(g_z.at[z], g_z.at[z], gz_s.at[t], gz_r.at[t], column(t))

    def gz_wait(t):
        f = column_from(t)
        remote(g_z.at[f], g_z.at[f], gz_s.at[t], gz_r.at[t], column(t)).wait_recv()

    start_all(1, 8, gz_send)
    p_step(4)
    for t in range(8):
        first = (9 * t) // 2
        skip = t % 2
        for i in range(4):
            p[8 * (first + skip) : 8 * (first + 5), BLOCK * i : BLOCK * i + BLOCK] = p_all[t, i, 8 * skip :]
    for i in range(4):
        lanes = slice(BLOCK * i, BLOCK * i + BLOCK)
        w_part[4 * i : 4 * i + 4] = dot_split(split(p[:, lanes]), (a_h[...], a_l[...]), 0, 0).reshape(4, 2, 16, COLS)
    w_swap = remote(w_part.at[:, 1 - c], w_comb, wc_s.at[0], wc_r.at[0], sibling)
    start_all(0, 1, lambda t: w_swap)

    loop(1, 8, gz_wait)
    strip = g_z[0]
    for t in range(1, 8):
        strip = strip + g_z[t]
    g_all[pl.ds(xy, 1), pl.ds(c, 1)] = strip.reshape(1, 1, STRIP, BLOCK)

    def ga_send(t):
        return remote(g_all.at[xy, c], g_all.at[xy, c], ga_s.at[t], ga_r.at[t], plane(t))

    def ga_wait(t):
        f = plane_from(t)
        remote(g_all.at[f, c], g_all.at[f, c], ga_s.at[t], ga_r.at[t], plane(t)).wait_recv()

    start_all(1, 16, ga_send)

    w_swap.wait_recv()
    w_half[...] = w_part[:, pl.ds(c, 1)].reshape(16, 16, COLS) + w_comb[...]

    def w_send(t):
        tx, ty, _, _ = plane(t)
        return remote(w_half.at[tx * 4 + ty], w_got.at[t], wr_s.at[t], wr_r.at[t], plane(t))

    def w_wait(t):
        remote(w_got.at[t], w_got.at[t], wr_s.at[t], wr_r.at[t], plane(t)).wait_recv()

    start_all(1, 16, w_send)
    loop(1, 16, ga_wait)
    g_forward = remote(g_all.at[:, c], g_all.at[:, c], gf_s.at[0], gf_r.at[0], sibling)
    start_all(0, 1, lambda t: g_forward)

    remote(g_all.at[:, 1 - c], g_all.at[:, 1 - c], gf_s.at[0], gf_r.at[0], sibling).wait_recv()
    for n, (i, j) in enumerate(PAIRS):
        for k in range(16):
            t = 16 * n + k
            o, e = divmod(t, 5)
            m[BLOCK * i + 8 * k : BLOCK * i + 8 * k + 8, BLOCK * j : BLOCK * j + BLOCK] = g_all[
                o // 2, o % 2, 8 * e : 8 * e + 8
            ]

    w_gather = PlaneGather(lambda h, xi, yi: w_all.at[xi, yi, c, half_rows(h)], wa_s, wa_r)

    def w_own():
        loop(1, 16, w_wait)
        own = w_half[pl.ds(xy, 1)].reshape(16, COLS)
        for t in range(1, 16):
            own = own + w_got[t]
        w_all[pl.ds(x, 1), pl.ds(y, 1), pl.ds(c, 1)] = own.reshape(1, 1, 1, 16, COLS)

    def w_column(h, k, v):
        u = wrap4(w_gather.origin(h, k))
        block = w_all.at[u, :, v, half_rows(h)] if h == 0 else w_all.at[:, u, v, half_rows(h)]
        return remote(block, block, wf_s.at[4 * h + k], wf_r.at[4 * h + k], sibling)

    def w_share():
        for k in range(4):
            w_gather.last(k)
            for h in range(2):
                start_all(0, 1, lambda t, h=h, k=k: w_column(h, k, c))

    def w_first():
        w_own()
        w_gather.first()

    hooks = {WHEN[0]: w_first, WHEN[1]: w_gather.middle, WHEN[2]: w_share}
    inv_chol(m, hooks)

    for i in range(4):
        lanes = slice(BLOCK * i, BLOCK * i + BLOCK)
        q[:, lanes] = dot(p[:, : BLOCK * i + BLOCK], m[lanes, : BLOCK * i + BLOCK], 1, 1)
    for k in range(4):
        for h in range(2):
            w_column(h, k, 1 - c).wait_recv()
    ones = jnp.ones((8, BLOCK), jnp.float32)
    for i in range(4):
        rows, known = slice(BLOCK * i, BLOCK * i + BLOCK), slice(0, BLOCK * i + BLOCK)
        w_h[rows], w_l[rows] = split(w_all[i].reshape(BLOCK, COLS))
        block = dot_split(split(m[rows, known]), (w_h[known], w_l[known]), 1, 0)
        s[8 * i : 8 * i + 8] = block.reshape(8, 16, COLS)
        square = block * block
        folded = square[:, :BLOCK]
        for k in range(1, 9):
            folded = folded + square[:, BLOCK * k : BLOCK * k + BLOCK]
        n_z[pl.ds(z, 1), :, rows] = dot(ones, folded, 1, 1).reshape(1, 8, BLOCK)

    def nz_send(t):
        return remote(n_z.at[z], n_z.at[z], nz_s.at[t], nz_r.at[t], column(t))

    def nz_wait(t):
        f = column_from(t)
        remote(n_z.at[f], n_z.at[f], nz_s.at[t], nz_r.at[t], column(t)).wait_recv()

    start_all(1, 8, nz_send)
    w_h[...], w_l[...] = split(s[...].reshape(RANK, COLS))
    new_momentum[...] = a[...] - (1.0 - MU) * dot_split(split(q[...]), (w_h[...], w_l[...]), 1, 0)
    loop(1, 8, nz_wait)
    squares = n_z[0]
    for t in range(1, 8):
        squares = squares + n_z[t]
    root = jnp.sqrt(squares / N_COLS + EPS)
    update[...] = dot_split(split(q[...] * (1.0 / root[:1])), (w_h[...], w_l[...]), 1, 0).astype(jnp.bfloat16)
    for i in range(4):
        turned = jnp.broadcast_to(root[:1, BLOCK * i : BLOCK * i + BLOCK], (BLOCK, BLOCK)).T
        roots[8 * i : 8 * i + 8] = turned.reshape(8, 16, BLOCK)
    mine = xy * 2 + c
    scale = roots[pl.ds(mine, 1)].reshape(16, BLOCK)
    strip = s[pl.ds(mine, 1)].reshape(16, COLS)
    for k in range(9):
        new_right[:, BLOCK * k : BLOCK * k + BLOCK] = strip[:, BLOCK * k : BLOCK * k + BLOCK] / scale

    finish()


WHEN = ((1, 4), (2, 4), (3, 6))


def per_device(momentum, gradient, right_factor):
    f32 = jnp.float32
    vmem, sem = pltpu.VMEM, pltpu.SemaphoreType.DMA
    scratch = [
        vmem((ROWS, COLS), f32), vmem((ROWS, COLS), jnp.bfloat16), vmem((ROWS, COLS), f32),
        vmem((ROWS, COLS), jnp.bfloat16), vmem((ROWS, COLS), jnp.bfloat16),
        vmem((4, 4, 2, 16, COLS), f32), vmem((4, ROWS, BLOCK), f32), vmem((2, 4, 4, STRIP, BLOCK), f32),
        vmem((8, 4, STRIP, BLOCK), f32),
        vmem((16, 2, STRIP, BLOCK), f32), vmem((16, STRIP, BLOCK), f32), vmem((16, STRIP, BLOCK), f32),
        vmem((16, STRIP, BLOCK), f32), vmem((8, STRIP, BLOCK), f32), vmem((16, 2, STRIP, BLOCK), f32),
        vmem((RANK, RANK), f32),
        vmem((16, 2, 16, COLS), f32), vmem((16, 16, COLS), f32), vmem((16, 16, COLS), f32),
        vmem((16, 16, COLS), f32),
        vmem((RANK, COLS), jnp.bfloat16), vmem((RANK, COLS), jnp.bfloat16), vmem((4, 4, 2, 16, COLS), f32),
        vmem((32, 16, COLS), f32),
        vmem((ROWS, RANK), f32), vmem((ROWS, RANK), f32), vmem((8, 8, RANK), f32), vmem((32, 16, BLOCK), f32),
        sem((3,)), sem((30,)), sem((30,)), sem((8,)), sem((8,)), sem((2, 4, 4)), sem((2, 4, 4)),
        sem((2, 4, 2)), sem((2, 4, 2)),
        sem((1,)), sem((1,)), sem((16,)), sem((16,)), sem((8,)), sem((8,)), sem((16,)), sem((16,)),
        sem((1,)), sem((1,)),
        sem((1,)), sem((1,)), sem((16,)), sem((16,)), sem((30,)), sem((30,)), sem((8,)), sem((8,)),
        sem((8,)), sem((8,)),
    ]
    return pl.pallas_call(
        step_kernel,
        out_shape=(
            jax.ShapeDtypeStruct((ROWS, COLS), f32),
            jax.ShapeDtypeStruct((16, COLS), f32),
            jax.ShapeDtypeStruct((ROWS, COLS), jnp.bfloat16),
        ),
        in_specs=[pl.BlockSpec(memory_space=pl.ANY)] * 3,
        out_specs=[pl.BlockSpec(memory_space=pltpu.VMEM)] * 3,
        scratch_shapes=scratch,
        compiler_params=pltpu.CompilerParams(
            collective_id=0, has_side_effects=True, vmem_limit_bytes=60 << 20
        ),
    )(momentum, gradient, right_factor)


def solution(mesh):
    finer = Mesh(
        mesh.devices.reshape(4, 4, 2, mesh.shape["narrow"]),
        ("wide_0", "wide_1", "wide_2", "narrow"),
    )
    return jax.shard_map(
        per_device,
        mesh=finer,
        in_specs=(P(WIDE, "narrow"), P(WIDE, "narrow"), P(WIDE, "narrow")),
        out_specs=(P(WIDE, "narrow"), P(WIDE, "narrow"), P(WIDE, "narrow")),
        check_vma=False,
    )
```
